32 devices in a mesh: row: 4 (over y, x), col: 4 (over z), depth: 2 (over core).
Axes of the slice: x: 2, y: 2, z: 4, core: 2. Of those that a mesh axis runs over, the one named last changes fastest.
Arguments:
- matrix_panel: bfloat16 [12288, 65536], P('row', 'col'), may hold values from -0.1484375 to 0.1484375
- start_block: bfloat16 [12288, 64], P('row', 'depth'), may hold values from -6 to 6
- stored_basis: float32 [12288, 1024], P('row'), may hold values from -2.2 to 2.2
Outputs:
- new_block: float32 [12288, 64], P('row', 'depth')
- coefficients: float32 [1024, 64], P(None, 'depth')
- triangle: float32 [64, 64], replicated
The draws below stay inside these ranges and needn't reach their ends.
All inputs are finite; a program needn't handle non-finite values.
Results may differ from the reference program's by a relative error of at most 0.0023.
Values may be sent and summed in bfloat16 or wider, within the bound.
A program may use at most 256 MiB of HBM per device.

```python
import jax
import jax.numpy as jnp
from jax import lax

N = 65536
K = 1024
B = 64
M = 12288


def basis_values(key):
    key_signs, key_codes, key_noise = jax.random.split(jax.random.fold_in(key, 23), 3)
    row_ids = jnp.arange(M, dtype=jnp.int32)[:, None]
    codes = jax.random.permutation(key_codes, K).astype(jnp.int32)[None, :]
    shared = jnp.bitwise_and(row_ids, codes)
    parity = jnp.zeros((M, K), jnp.int32)
    for shift_count in range(24):
        parity = parity + jnp.bitwise_and(jnp.right_shift(shared, shift_count), 1)
    parity = jnp.bitwise_and(parity, 1)
    row_signs = jax.random.randint(key_signs, (M, 1), 0, 2).astype(jnp.int32) * 2 - 1
    walsh = (row_signs * (1 - 2 * parity)).astype(jnp.float32)
    noise = 0.2 * jnp.clip(jax.random.normal(key_noise, (M, K)), -6.0, 6.0)
    return (walsh + noise).astype(jnp.float32)


def draw_matrix_panel(key, part):
    key_noise, key_rows, key_cols, key_mix = jax.random.split(jax.random.fold_in(key, 11), 4)
    basis = basis_values(key)
    position = jnp.arange(M, dtype=jnp.float32)[:, None] / (M - 1)
    row_factor = jnp.exp(0.6 * jax.random.uniform(key_rows, (M, 1), minval=-1.0, maxval=1.0)) * jnp.sqrt(1.0 + position)
    col_factor = jnp.exp(jnp.log(10.0) * (jax.random.uniform(key_cols, (1, N)) - 0.5))
    mix_values = jnp.clip(jax.random.normal(key_mix, (K, N)), -6.0, 6.0)
    coupling = 2.2 * (float(N + M) / float(K)) ** 0.25 / float(N * M) ** 0.5
    mix_values = (mix_values * col_factor * coupling).astype(jnp.float32)
    noise_scale = 1.0 / (2.0 * float(N * M) ** 0.25)

    def block_rows(block_index):
        first_row = (block_index * K).astype(jnp.int32)
        block_key = jax.random.fold_in(key_noise, block_index)
        noise = jnp.clip(jax.random.normal(block_key, (K, N)), -6.0, 6.0)
        rows_scale = lax.dynamic_slice_in_dim(row_factor, first_row, K, 0)
        rows_basis = lax.dynamic_slice_in_dim(basis, first_row, K, 0)
        along = jnp.dot(rows_basis, mix_values, precision=lax.Precision.HIGHEST, preferred_element_type=jnp.float32)
        values = noise * rows_scale * col_factor * noise_scale + along
        values = jnp.clip(values, -0.1484375, 0.1484375)
        return values.astype(jnp.bfloat16)
    blocks = lax.map(block_rows, jnp.arange(M // K, dtype=jnp.int32))
    return blocks.reshape(M, N)


def draw_stored_basis(key, part):
    return basis_values(key)


def shard_levels(own_key, shape, cuts, low, high):
    def one(dim, shards_of):
        steps = jax.random.uniform(jax.random.fold_in(jax.random.fold_in(own_key, 6), dim), (shards_of,), jnp.float32, low / len(cuts), high / len(cuts))
        return jnp.repeat(jnp.exp(steps), shape[dim] // shards_of).reshape((-1,) + (1,) * (len(shape) - dim - 1))

    gain = one(*cuts[0])
    for cut in cuts[1:]:
        gain = gain * one(*cut)
    return gain


def centred(rng, shape, scale, most, cuts=(), kind=jnp.bfloat16):
    result = jax.random.normal(rng, shape, jnp.float32) * scale
    if len(cuts) > 0:
        result = shard_levels(rng, shape, cuts, -0.22, 0.18) * result
    return jnp.clip(result, min=-most, max=most).astype(kind)


def setup_inputs(seed: int = 0) -> dict:
    key_list = jax.random.split(jax.random.key(seed), 4)
    matrix_panel = draw_matrix_panel(jax.random.fold_in(key_list[3], 71), 0)
    start_block = centred(key_list[1], (M, B), 1.0, 6.0, ((0, 4), (1, 2)))
    stored_basis = draw_stored_basis(jax.random.fold_in(key_list[3], 71), 0)
    return dict(matrix_panel=matrix_panel, start_block=start_block, stored_basis=stored_basis)


HIGHEST = lax.Precision.HIGHEST

def factor_gram(gram_matrix):
    lower_factor = jnp.linalg.cholesky(gram_matrix)
    identity = jnp.eye(gram_matrix.shape[0], dtype=jnp.float32)
    inverse = jax.scipy.linalg.solve_triangular(lower_factor, identity, lower=True)
    return (lower_factor, inverse)

def orthonormal_pass(stored_basis, block_cols):
    projection = jnp.dot(stored_basis.T.astype(jnp.float32), block_cols.astype(jnp.float32), precision=HIGHEST, preferred_element_type=jnp.float32) / M
    remainder = block_cols - jnp.dot(stored_basis.astype(jnp.float32), projection.astype(jnp.float32), precision=HIGHEST, preferred_element_type=jnp.float32)
    gram_matrix = jnp.dot(remainder.T.astype(jnp.float32), remainder.astype(jnp.float32), precision=HIGHEST, preferred_element_type=jnp.float32) / M
    lower_factor, inverse = factor_gram(gram_matrix)
    normed = jnp.dot(remainder.astype(jnp.float32), inverse.T.astype(jnp.float32), precision=HIGHEST, preferred_element_type=jnp.float32)
    return (projection, lower_factor, normed)

def reference(matrix_panel, start_block, stored_basis):
    mixed_cols = jnp.dot(matrix_panel.T.astype(jnp.float32), start_block.astype(jnp.float32), preferred_element_type=jnp.float32).astype(jnp.bfloat16)
    image_block = jnp.dot(matrix_panel.astype(jnp.float32), mixed_cols.astype(jnp.float32), preferred_element_type=jnp.float32)
    proj_first, lower_first, normed_first = orthonormal_pass(stored_basis, image_block)
    proj_second, lower_second, new_block = orthonormal_pass(stored_basis, normed_first)
    coefficients = proj_first + jnp.dot(proj_second.astype(jnp.float32), lower_first.T.astype(jnp.float32), precision=HIGHEST, preferred_element_type=jnp.float32)
    triangle = jnp.dot(lower_second.T.astype(jnp.float32), lower_first.T.astype(jnp.float32), precision=HIGHEST, preferred_element_type=jnp.float32)
    return (new_block, coefficients, triangle)
```

```python
import functools

import jax
import jax.numpy as jnp
from jax import lax
from jax.experimental import pallas as pl
from jax.experimental.pallas import tpu as pltpu
from jax.sharding import PartitionSpec as P

HIGHEST = lax.Precision.HIGHEST
HIGH = lax.Precision.HIGH
MESH = pl.DeviceIdType.MESH
F32 = jnp.float32
LANES = 128
LAG_SUM = 5
LAG_USE = 10
LATE = 2


def mm(a, b, precision=HIGHEST):
    return lax.dot_general(
        a, b, (((1,), (0,)), ((), ())), precision=precision, preferred_element_type=F32
    )


def mm_nt(a, b, precision=HIGHEST):
    return lax.dot_general(
        a, b, (((1,), (1,)), ((), ())), precision=precision, preferred_element_type=F32
    )


def factor(gram_twice):
    size = gram_twice.shape[0]
    rows = lax.broadcasted_iota(jnp.int32, (size, 2 * size), 0)
    lanes = lax.broadcasted_iota(jnp.int32, (size, 2 * size), 1)
    work = jnp.where(lanes < size, gram_twice, jnp.where(lanes - size == rows, 1.0, 0.0))

    def all_sum(mask, value):
        part_sum = jnp.sum(jnp.where(mask, value, 0.0), axis=0, keepdims=True)
        return jnp.sum(part_sum, axis=1, keepdims=True)

    def step(i, carry):
        work, pivots = carry
        k = 2 * i
        n = k + 1
        lane_k, lane_n = lanes == k, lanes == n
        row_is_k, row_is_n = rows == k, rows == n
        column_k = jnp.sum(jnp.where(lane_k, work, 0.0), axis=1, keepdims=True)
        column_n = jnp.sum(jnp.where(lane_n, work, 0.0), axis=1, keepdims=True)
        row_k = jnp.sum(jnp.where(row_is_k, work, 0.0), axis=0, keepdims=True)
        row_n = jnp.sum(jnp.where(row_is_n, work, 0.0), axis=0, keepdims=True)
        pivot_k = all_sum(row_is_k & lane_k, work)
        upper = all_sum(row_is_k & lane_n, work)
        lower = all_sum(row_is_n & lane_k, work)
        corner = all_sum(row_is_n & lane_n, work)
        ratio = lower / pivot_k
        pivot_n = corner - ratio * upper
        row_n = row_n - ratio * row_k
        scale_k = column_k / pivot_k
        scale_n = (column_n - scale_k * upper) / pivot_n
        work = work - jnp.where(rows > k, scale_k * row_k, 0.0)
        work = work - jnp.where(rows > n, scale_n * row_n, 0.0)
        pivots = jnp.where(row_is_k, pivot_k, jnp.where(row_is_n, pivot_n, pivots))
        return (work, pivots)

    work, pivots = lax.fori_loop(0, size // 2, step, (work, jnp.ones_like(work)))
    work = work / jnp.sqrt(pivots)
    upper = jnp.where(rows <= lanes, work, 0.0)[:, :size]
    return (upper, work[:, size:])


def encode(value):
    return (value * jnp.abs(value)).astype(jnp.bfloat16)


def decode(code):
    code = code.astype(F32)
    return code * lax.rsqrt(jnp.maximum(jnp.abs(code), 1e-37))


def krylov_kernel(
    dims,
    panel_ref,
    start_ref,
    basis_ref,
    new_ref,
    coef_ref,
    tri_ref,
    held,
    start_all,
    fresh,
    own,
    part,
    landed,
    gathered,
    image,
    sib_buf,
    col_buf,
    basis,
    pair_out,
    pair_in,
    proj_part,
    proj_in,
    proj_all,
    half_out,
    half_in,
    gram_out,
    gram_pair,
    gram_all,
    gram_half,
    gram_back,
    panel_sem,
    misc_sem,
    sib_sem,
    r_send,
    r_recv,
    b_send,
    b_recv,
    half_send,
    half_recv,
    col_send,
    col_recv,
    pair_send,
    pair_recv,
    p_send,
    p_recv,
    a_send,
    a_recv,
    g_send,
    g_recv,
    o_send,
    o_recv,
    s_send,
    s_recv,
):
    n_row, n_col, total_rows = dims
    chunks, rows_here, width = held.shape
    cols = start_all.shape[0] * start_all.shape[1]
    half = cols // 2
    pieces = image.shape[0]
    piece = image.shape[2]
    n_chip = n_row * n_col
    row = lax.axis_index("row")
    col = lax.axis_index("col")
    core = lax.axis_index("depth")
    inv_total = 1.0 / total_rows
    chip_me = row * n_col + col
    sibling = {"depth": 1 - core}

    def chip_device(j):
        target = (chip_me + j) % n_chip
        return target, {"row": target // n_col, "col": target % n_col}

    def col_device(j):
        target = (col + j) % n_col
        return target, {"col": target}

    def row_device(j):
        target = (row + j) % n_row
        return target, {"row": target}

    def panel_copy(t):
        first = pl.multiple_of((core * chunks + t) * width, width)
        return pltpu.make_async_copy(
            panel_ref.at[:, pl.ds(first, width)], held.at[t], panel_sem.at[t]
        )

    own_start = pltpu.make_async_copy(start_ref, start_all.at[core], misc_sem.at[1])
    own_start.start()
    for t in range(chunks):
        panel_copy(t).start()
    basis_first = pl.multiple_of((core * n_col + col) * piece, 8)
    basis_copy = pltpu.make_async_copy(
        basis_ref.at[pl.ds(basis_first, piece), :], basis, misc_sem.at[0]
    )
    basis_copy.start()

    barrier = pltpu.get_barrier_semaphore()
    greeted = [row_device(j)[1] for j in range(1, n_row)]
    greeted += [col_device(j)[1] for j in range(1, n_col)] + [sibling]
    for device in greeted:
        pl.semaphore_signal(barrier, inc=1, device_id=device, device_id_type=MESH)
    pl.semaphore_wait(barrier, len(greeted))

    def remote(src, dst, send_sem, recv_sem, device):
        return pltpu.make_async_remote_copy(
            src_ref=src,
            dst_ref=dst,
            send_sem=send_sem,
            recv_sem=recv_sem,
            device_id=device,
            device_id_type=MESH,
        )

    start_copy = remote(start_ref, start_all.at[core], sib_sem.at[0], sib_sem.at[1], sibling)
    start_copy.start()
    image[...] = jnp.zeros_like(image)
    own_start.wait()
    start_copy.wait()

    def reduce_copy(j, t):
        target, device = row_device(j)
        return remote(
            part.at[t, target], landed.at[t, row], r_send.at[j, t], r_recv.at[j, t], device
        )

    def gather_copy(j, t):
        region = gathered.at[t, row]
        return remote(region, region, b_send.at[j, t], b_recv.at[j, t], row_device(j)[1])

    def multiply(i):
        panel_copy(i).wait()
        mixed = mm(start_all[...].reshape(cols, rows_here), held[i], None)
        for p in range(n_row):
            lanes = mixed[:, p * LANES : (p + 1) * LANES]
            fresh[p] = lanes
            part[i, p] = encode(lanes)
        for j in range(1, n_row):
            reduce_copy(j, i).start()
        own[i] = fresh[row]

    def combine(t):
        for j in range(1, n_row):
            reduce_copy(j, t).wait_recv()
        summed = own[t]
        for j in range(1, n_row):
            summed = summed + decode(landed[t, (row + j) % n_row])
        gathered[t, row] = summed.astype(jnp.bfloat16)
        for j in range(1, n_row):
            gather_copy(j, t).start()

    block = rows_here // 4
    per_block = block // piece

    def mixed_of(t):
        for j in range(1, n_row):
            gather_copy(j, t).wait_recv()
        return jnp.concatenate([gathered[t, p] for p in range(n_row)], axis=1)

    def apply(t):
        lhs = mixed_of(t)
        for h in range(4):
            got = mm_nt(lhs, held[t, h * block : (h + 1) * block, :], None)
            for q in range(per_block):
                image[h * per_block + q] += got[:, q * piece : (q + 1) * piece]

    early = chunks - LATE
    cuts = sorted({0, LAG_SUM, LAG_USE, chunks, chunks + LAG_SUM, early + LAG_USE})
    for first, last in zip(cuts[:-1], cuts[1:]):

        def body(i, carry, first=first):
            if LAG_SUM <= first < chunks + LAG_SUM:
                combine(i - LAG_SUM)
            if first < chunks:
                multiply(i)
            if LAG_USE <= first:
                apply(i - LAG_USE)
            return carry

        lax.fori_loop(first, last, body, 0)

    def half_copy(c):
        return remote(
            image.at[(1 - core) * n_col + c], sib_buf.at[c], half_send.at[c], half_recv.at[c], sibling
        )

    late = [(t, mixed_of(t)) for t in range(early, chunks)]

    def finish_piece(index):
        first = pl.multiple_of(index * piece, 16)
        got = image[index]
        for t, lhs in late:
            got = got + mm_nt(lhs, held[t, pl.ds(first, piece), :], None)
        image[index] = got

    for j in range(1, n_col + 1):
        target = (col + j) % n_col
        finish_piece((1 - core) * n_col + target)
        half_copy(target).start()
    copies = []
    for j in range(1, n_col):
        target, device = col_device(j)
        finish_piece(core * n_col + target)
        half_copy(target).wait_recv()
        sib_buf[target] = sib_buf[target] + image[core * n_col + target]
        copies.append(
            remote(sib_buf.at[target], col_buf.at[col], col_send.at[j], col_recv.at[j], device)
        )
        copies[-1].start()
    finish_piece(core * n_col + col)
    half_copy(col).wait_recv()
    col_buf[col] = sib_buf[col] + image[core * n_col + col]

    def drain(t, carry):
        for j in range(1, n_row):
            reduce_copy(j, t).wait_send()
            gather_copy(j, t).wait_send()
        return carry

    lax.fori_loop(0, chunks, drain, 0)
    for c in range(n_col):
        half_copy(c).wait_send()
    basis_copy.wait()
    for copy in copies:
        copy.wait()

    image_t = col_buf[0]
    for c in range(1, n_col):
        image_t = image_t + col_buf[c]

    piece_rows, piece_lanes = proj_part.shape[1:]
    lane_blocks = basis.shape[1] // piece_lanes

    def finish(made):
        for copy in made:
            copy.wait()

    def start_chips(slot, src_of, dst, send, recv):
        made = []
        for j in range(1, n_chip):
            target, device = chip_device(j)
            made.append(remote(src_of(target), dst, send.at[slot, j], recv.at[slot, j], device))
            made[-1].start()
        return made

    def chip_sum(ref, slot):
        total = ref[slot, 0]
        for c in range(1, n_chip):
            total = total + ref[slot, c]
        return total

    def project(slot, value):
        partial = mm(value, basis[...], HIGH)
        pair_out[slot, 0] = partial[:half]
        pair_out[slot, 1] = partial[half:]
        swap = remote(
            pair_out.at[slot, 1 - core], pair_in.at[slot],
            pair_send.at[slot], pair_recv.at[slot], sibling,
        )
        swap.start()
        swap.wait()
        both = pair_out[slot, core] + pair_in[slot]
        for p in range(n_chip):
            lane = (p % lane_blocks) * piece_lanes
            top = (p // lane_blocks) * piece_rows
            proj_part[p] = both[top : top + piece_rows, lane : lane + piece_lanes]
        copies = start_chips(
            slot, lambda target: proj_part.at[target], proj_in.at[slot, chip_me], p_send, p_recv
        )
        proj_in[slot, chip_me] = proj_part[chip_me]
        finish(copies)
        proj_all[slot, chip_me] = chip_sum(proj_in, slot) * inv_total
        mine = proj_all.at[slot, chip_me]
        finish(start_chips(slot, lambda target: mine, mine, a_send, a_recv))
        bands = []
        for top in range(n_chip // lane_blocks):
            bands.append(
                jnp.concatenate(
                    [proj_all[slot, top * lane_blocks + p] for p in range(lane_blocks)], axis=1
                )
            )
        half_out[slot] = jnp.concatenate(bands, axis=0) if len(bands) > 1 else bands[0]
        swap = remote(
            half_out.at[slot], half_in.at[slot],
            pair_send.at[2 + slot], pair_recv.at[2 + slot], sibling,
        )
        swap.start()
        swap.wait()
        lower, upper = half_out[slot], half_in[slot]
        low = jnp.where(core == 0, lower, upper)
        high = jnp.where(core == 0, upper, lower)
        return jnp.concatenate([low, high], axis=0)

    def pack(value):
        return jnp.concatenate([value[: half // 2], value[half // 2 :]], axis=1)

    def gram_sum(value, beside, after):
        local = mm_nt(value, value)
        gram_out[0] = pack(local[:half])
        gram_out[1] = pack(local[half:])
        swap = remote(
            gram_out.at[1 - core], gram_pair, pair_send.at[4], pair_recv.at[4], sibling
        )
        swap.start()
        swap.wait()
        gram_all[0, chip_me] = gram_out[core] + gram_pair[...]
        mine = gram_all.at[0, chip_me]
        gram_copies = start_chips(0, lambda target: mine, mine, g_send, g_recv)
        beside()
        finish(gram_copies)
        gram_half[...] = chip_sum(gram_all, 0) * inv_total
        swap = remote(gram_half, gram_back, pair_send.at[5], pair_recv.at[5], sibling)
        swap.start()
        after()
        swap.wait()
        low = jnp.where(core == 0, gram_half[...], gram_back[...])
        high = jnp.where(core == 0, gram_back[...], gram_half[...])
        return jnp.concatenate([low[:, :cols], low[:, cols:], high[:, :cols], high[:, cols:]], axis=0)

    proj_first = project(0, image_t)
    remainder = image_t - mm_nt(proj_first, basis[...], HIGH)
    proj_second = project(1, remainder)
    second = remainder - mm_nt(proj_second, basis[...], HIGH)
    group = core * n_col + col
    second_copies = []
    pair_copies = []

    def spread():
        image[group] = second
        for j in range(1, n_col):
            mine = image.at[group]
            second_copies.append(
                remote(mine, mine, s_send.at[j], s_recv.at[j], col_device(j)[1])
            )
            second_copies[-1].start()
        coef = proj_first + proj_second
        coef_ref[...] = jnp.where(core == 0, coef[:half], coef[half:])

    def share():
        finish(second_copies)
        for c in range(n_col):
            region = image.at[core * n_col + c]
            pair_copies.append(remote(region, region, o_send.at[c], o_recv.at[c], sibling))
            pair_copies[-1].start()

    gram = gram_sum(second, spread, share)
    upper, inverse = factor(jnp.concatenate([gram, gram], axis=1))
    tri_ref[...] = upper
    own_rows = jnp.where(core == 0, inverse[:half], inverse[half:])
    finish(pair_copies)
    for q in range(pieces):
        new_ref[:, q * piece : (q + 1) * piece] = mm(own_rows, image[q])


def hand_over(new_in, coef_in, tri_in, new_ref, coef_ref, tri_ref):
    new_ref[...] = new_in[...]
    coef_ref[...] = coef_in[...]
    tri_ref[...] = tri_in[...]


def per_device(matrix_panel, start_block, stored_basis):
    n_row = lax.axis_size("row")
    n_col = lax.axis_size("col")
    n_core = lax.axis_size("depth")
    rows_here, cols_here = matrix_panel.shape
    half = start_block.shape[1]
    cols = half * n_core
    k_total = stored_basis.shape[1]
    width = LANES * n_row
    chunks = cols_here // n_core // width
    pieces = n_col * n_core
    piece = rows_here // pieces
    n_chip = n_row * n_col
    piece_lanes = LANES
    piece_rows = half * k_total // (n_chip * piece_lanes)
    dma = pltpu.SemaphoreType.DMA
    bf16 = jnp.bfloat16
    scratch = [
        pltpu.VMEM((chunks, rows_here, width), bf16),
        pltpu.VMEM((n_core, half, rows_here), bf16),
        pltpu.VMEM((n_row, cols, LANES), F32),
        pltpu.VMEM((chunks, cols, LANES), F32),
        pltpu.VMEM((chunks, n_row, cols, LANES), bf16),
        pltpu.VMEM((chunks, n_row, cols, LANES), bf16),
        pltpu.VMEM((chunks, n_row, cols, LANES), bf16),
        pltpu.VMEM((pieces, cols, piece), F32),
        pltpu.VMEM((n_col, cols, piece), F32),
        pltpu.VMEM((n_col, cols, piece), F32),
        pltpu.VMEM((piece, k_total), F32),
        pltpu.VMEM((2, n_core, half, k_total), F32),
        pltpu.VMEM((2, half, k_total), F32),
        pltpu.VMEM((n_chip, piece_rows, piece_lanes), F32),
        pltpu.VMEM((2, n_chip, piece_rows, piece_lanes), F32),
        pltpu.VMEM((2, n_chip, piece_rows, piece_lanes), F32),
        pltpu.VMEM((2, half, k_total), F32),
        pltpu.VMEM((2, half, k_total), F32),
        pltpu.VMEM((n_core, half // 2, 2 * cols), F32),
        pltpu.VMEM((half // 2, 2 * cols), F32),
        pltpu.VMEM((1, n_chip, half // 2, 2 * cols), F32),
        pltpu.VMEM((half // 2, 2 * cols), F32),
        pltpu.VMEM((half // 2, 2 * cols), F32),
        dma((chunks,)),
        dma((2,)),
        dma((2,)),
    ]
    scratch += [dma((n_row, chunks))] * 4
    scratch += [dma((n_col,))] * 4
    scratch += [dma((6,))] * 2
    scratch += [dma((2, n_chip))] * 4
    scratch += [dma((1, n_chip))] * 2
    scratch += [dma((n_col,))] * 4
    whole = pl.BlockSpec(memory_space=pltpu.VMEM)
    hbm = pl.BlockSpec(memory_space=pl.ANY)
    shapes = (
        jax.ShapeDtypeStruct((half, rows_here), F32),
        jax.ShapeDtypeStruct((half, k_total), F32),
        jax.ShapeDtypeStruct((cols, cols), F32),
    )
    made = pl.pallas_call(
        functools.partial(krylov_kernel, (n_row, n_col, rows_here * n_row)),
        out_shape=shapes,
        in_specs=[hbm, whole, hbm],
        out_specs=(whole, whole, whole),
        scratch_shapes=scratch,
        compiler_params=pltpu.CompilerParams(
            collective_id=0, has_side_effects=True, vmem_limit_bytes=63 << 20
        ),
    )(matrix_panel, start_block.T, stored_basis)
    new_t, coef_t, triangle = pl.pallas_call(
        hand_over,
        out_shape=shapes,
        in_specs=[whole, whole, whole],
        out_specs=(whole, whole, whole),
    )(*made)
    return (new_t.T, coef_t.T, triangle)


def solution(mesh):
    placed = (P("row", "col"), P("row", "depth"), P("row", None))
    return jax.shard_map(
        per_device,
        mesh=mesh,
        in_specs=placed,
        out_specs=(P("row", "depth"), P(None, "depth"), P()),
        check_vma=False,
    )
```

```python
import functools

import jax
import jax.numpy as jnp
from jax import lax
from jax.experimental import pallas as pl
from jax.experimental.pallas import tpu as pltpu
from jax.sharding import PartitionSpec as P

HIGHEST = lax.Precision.HIGHEST
HIGH = lax.Precision.HIGH
MESH = pl.DeviceIdType.MESH
F32 = jnp.float32
LANES = 128
LAG_SUM = 5
LAG_USE = 12
LATE = 4


def mm(a, b, precision=HIGHEST):
    return lax.dot_general(
        a, b, (((1,), (0,)), ((), ())), precision=precision, preferred_element_type=F32
    )


def mm_nt(a, b, precision=HIGHEST):
    return lax.dot_general(
        a, b, (((1,), (1,)), ((), ())), precision=precision, preferred_element_type=F32
    )


def factor(gram_twice):
    size = gram_twice.shape[0]
    rows = lax.broadcasted_iota(jnp.int32, (size, 2 * size), 0)
    lanes = lax.broadcasted_iota(jnp.int32, (size, 2 * size), 1)
    work = jnp.where(lanes < size, gram_twice, jnp.where(lanes - size == rows, 1.0, 0.0))

    def all_sum(mask, value):
        part_sum = jnp.sum(jnp.where(mask, value, 0.0), axis=0, keepdims=True)
        return jnp.sum(part_sum, axis=1, keepdims=True)

    def step(i, carry):
        work, pivots = carry
        k = 2 * i
        n = k + 1
        lane_k, lane_n = lanes == k, lanes == n
        row_is_k, row_is_n = rows == k, rows == n
        column_k = jnp.sum(jnp.where(lane_k, work, 0.0), axis=1, keepdims=True)
        column_n = jnp.sum(jnp.where(lane_n, work, 0.0), axis=1, keepdims=True)
        row_k = jnp.sum(jnp.where(row_is_k, work, 0.0), axis=0, keepdims=True)
        row_n = jnp.sum(jnp.where(row_is_n, work, 0.0), axis=0, keepdims=True)
        pivot_k = all_sum(row_is_k & lane_k, work)
        upper = all_sum(row_is_k & lane_n, work)
        lower = all_sum(row_is_n & lane_k, work)
        corner = all_sum(row_is_n & lane_n, work)
        ratio = lower / pivot_k
        pivot_n = corner - ratio * upper
        row_n = row_n - ratio * row_k
        scale_k = column_k / pivot_k
        scale_n = (column_n - scale_k * upper) / pivot_n
        work = work - jnp.where(rows > k, scale_k * row_k, 0.0)
        work = work - jnp.where(rows > n, scale_n * row_n, 0.0)
        pivots = jnp.where(row_is_k, pivot_k, jnp.where(row_is_n, pivot_n, pivots))
        return (work, pivots)

    work, pivots = lax.fori_loop(0, size // 2, step, (work, jnp.ones_like(work)))
    work = work / jnp.sqrt(pivots)
    upper = jnp.where(rows <= lanes, work, 0.0)[:, :size]
    return (upper, work[:, size:])


def encode(value):
    return (value * jnp.abs(value)).astype(jnp.bfloat16)


def decode(code):
    code = code.astype(F32)
    return code * lax.rsqrt(jnp.maximum(jnp.abs(code), 1e-37))


def krylov_kernel(
    dims,
    panel_ref,
    start_ref,
    basis_ref,
    new_ref,
    coef_ref,
    tri_ref,
    held,
    start_all,
    fresh,
    own,
    part,
    landed,
    gathered,
    image,
    sib_buf,
    col_buf,
    basis,
    pair_out,
    pair_in,
    proj_part,
    proj_in,
    proj_all,
    half_out,
    half_in,
    gram_out,
    gram_pair,
    gram_all,
    gram_half,
    gram_back,
    second_all,
    panel_sem,
    misc_sem,
    sib_sem,
    r_send,
    r_recv,
    b_send,
    b_recv,
    half_send,
    half_recv,
    col_send,
    col_recv,
    pair_send,
    pair_recv,
    p_send,
    p_recv,
    a_send,
    a_recv,
    g_send,
    g_recv,
    o_send,
    o_recv,
    s_send,
    s_recv,
):
    n_row, n_col, total_rows = dims
    chunks, rows_here, width = held.shape
    cols = start_all.shape[0] * start_all.shape[1]
    half = cols // 2
    pieces = image.shape[0]
    piece = image.shape[2]
    n_chip = n_row * n_col
    row = lax.axis_index("row")
    col = lax.axis_index("col")
    core = lax.axis_index("depth")
    inv_total = 1.0 / total_rows
    chip_me = row * n_col + col
    sibling = {"depth": 1 - core}

    def chip_device(j):
        target = (chip_me + j) % n_chip
        return target, {"row": target // n_col, "col": target % n_col}

    def col_device(j):
        target = (col + j) % n_col
        return target, {"col": target}

    def row_device(j):
        target = (row + j) % n_row
        return target, {"row": target}

    def panel_copy(t):
        first = pl.multiple_of((core * chunks + t) * width, width)
        return pltpu.make_async_copy(
            panel_ref.at[:, pl.ds(first, width)], held.at[t], panel_sem.at[t]
        )

    own_start = pltpu.make_async_copy(start_ref, start_all.at[core], misc_sem.at[1])
    own_start.start()
    for t in range(chunks):
        panel_copy(t).start()
    basis_first = pl.multiple_of((core * n_col + col) * piece, 8)
    basis_copy = pltpu.make_async_copy(
        basis_ref.at[pl.ds(basis_first, piece), :], basis, misc_sem.at[0]
    )
    basis_copy.start()

    barrier = pltpu.get_barrier_semaphore()
    greeted = [row_device(j)[1] for j in range(1, n_row)]
    greeted += [col_device(j)[1] for j in range(1, n_col)] + [sibling]
    for device in greeted:
        pl.semaphore_signal(barrier, inc=1, device_id=device, device_id_type=MESH)
    pl.semaphore_wait(barrier, len(greeted))

    def remote(src, dst, send_sem, recv_sem, device):
        return pltpu.make_async_remote_copy(
            src_ref=src,
            dst_ref=dst,
            send_sem=send_sem,
            recv_sem=recv_sem,
            device_id=device,
            device_id_type=MESH,
        )

    start_copy = remote(start_ref, start_all.at[core], sib_sem.at[0], sib_sem.at[1], sibling)
    start_copy.start()
    image[...] = jnp.zeros_like(image)
    own_start.wait()
    start_copy.wait()

    def reduce_copy(j, t):
        target, device = row_device(j)
        return remote(
            part.at[t, target], landed.at[t, row], r_send.at[j, t], r_recv.at[j, t], device
        )

    def gather_copy(j, t):
        region = gathered.at[t, row]
        return remote(region, region, b_send.at[j, t], b_recv.at[j, t], row_device(j)[1])

    def multiply(i):
        panel_copy(i).wait()
        mixed = mm(start_all[...].reshape(cols, rows_here), held[i], None)
        for p in range(n_row):
            lanes = mixed[:, p * LANES : (p + 1) * LANES]
            fresh[p] = lanes
            part[i, p] = encode(lanes)
        for j in range(1, n_row):
            reduce_copy(j, i).start()
        own[i] = fresh[row]

    def combine(t):
        for j in range(1, n_row):
            reduce_copy(j, t).wait_recv()
        summed = own[t]
        for j in range(1, n_row):
            summed = summed + decode(landed[t, (row + j) % n_row])
        gathered[t, row] = summed.astype(jnp.bfloat16)
        for j in range(1, n_row):
            gather_copy(j, t).start()

    block = rows_here // 4
    per_block = block // piece

    def mixed_of(t):
        for j in range(1, n_row):
            gather_copy(j, t).wait_recv()
        return jnp.concatenate([gathered[t, p] for p in range(n_row)], axis=1)

    def apply(t):
        lhs = mixed_of(t)
        for h in range(4):
            got = mm_nt(lhs, held[t, h * block : (h + 1) * block, :], None)
            for q in range(per_block):
                image[h * per_block + q] += got[:, q * piece : (q + 1) * piece]

    early = max(chunks - LATE, 0)
    cuts = sorted({0, LAG_SUM, LAG_USE, chunks, chunks + LAG_SUM, early + LAG_USE})
    for first, last in zip(cuts[:-1], cuts[1:]):

        def body(i, carry, first=first):
            if LAG_SUM <= first < chunks + LAG_SUM:
                combine(i - LAG_SUM)
            if first < chunks:
                multiply(i)
            if LAG_USE <= first:
                apply(i - LAG_USE)
            return carry

        lax.fori_loop(first, last, body, 0)

    def half_copy(c):
        return remote(
            image.at[(1 - core) * n_col + c], sib_buf.at[c], half_send.at[c], half_recv.at[c], sibling
        )

    late = [(t, mixed_of(t)) for t in range(early, chunks)]

    def finish_piece(index):
        first = pl.multiple_of(index * piece, 16)
        got = image[index]
        for t, lhs in late:
            got = got + mm_nt(lhs, held[t, pl.ds(first, piece), :], None)
        image[index] = got

    for j in range(1, n_col + 1):
        target = (col + j) % n_col
        finish_piece((1 - core) * n_col + target)
        half_copy(target).start()
    copies = []
    for j in range(1, n_col):
        target, device = col_device(j)
        finish_piece(core * n_col + target)
        half_copy(target).wait_recv()
        sib_buf[target] = sib_buf[target] + image[core * n_col + target]
        copies.append(
            remote(sib_buf.at[target], col_buf.at[col], col_send.at[j], col_recv.at[j], device)
        )
        copies[-1].start()
    finish_piece(core * n_col + col)
    half_copy(col).wait_recv()
    col_buf[col] = sib_buf[col] + image[core * n_col + col]

    def drain(t, carry):
        for j in range(1, n_row):
            reduce_copy(j, t).wait_send()
            gather_copy(j, t).wait_send()
        return carry

    lax.fori_loop(0, chunks, drain, 0)
    for c in range(n_col):
        half_copy(c).wait_send()
    basis_copy.wait()
    for copy in copies:
        copy.wait()

    image_t = col_buf[0]
    for c in range(1, n_col):
        image_t = image_t + col_buf[c]

    piece_rows, piece_lanes = proj_part.shape[1:]
    lane_blocks = basis.shape[1] // piece_lanes

    def finish(made):
        for copy in made:
            copy.wait()

    def start_chips(slot, src_of, dst, send, recv):
        made = []
        for j in range(1, n_chip):
            target, device = chip_device(j)
            made.append(remote(src_of(target), dst, send.at[slot, j], recv.at[slot, j], device))
            made[-1].start()
        return made

    def chip_sum(ref, slot):
        total = ref[slot, 0]
        for c in range(1, n_chip):
            total = total + ref[slot, c]
        return total

    def project(slot, value):
        partial = mm(value, basis[...], HIGH)
        pair_out[slot, 0] = partial[:half]
        pair_out[slot, 1] = partial[half:]
        swap = remote(
            pair_out.at[slot, 1 - core], pair_in.at[slot],
            pair_send.at[slot], pair_recv.at[slot], sibling,
        )
        swap.start()
        swap.wait()
        both = pair_out[slot, core] + pair_in[slot]
        for p in range(n_chip):
            lane = (p % lane_blocks) * piece_lanes
            top = (p // lane_blocks) * piece_rows
            proj_part[p] = both[top : top + piece_rows, lane : lane + piece_lanes]
        copies = start_chips(
            slot, lambda target: proj_part.at[target], proj_in.at[slot, chip_me], p_send, p_recv
        )
        proj_in[slot, chip_me] = proj_part[chip_me]
        finish(copies)
        proj_all[slot, chip_me] = chip_sum(proj_in, slot) * inv_total
        mine = proj_all.at[slot, chip_me]
        finish(start_chips(slot, lambda target: mine, mine, a_send, a_recv))
        bands = []
        for top in range(n_chip // lane_blocks):
            bands.append(
                jnp.concatenate(
                    [proj_all[slot, top * lane_blocks + p] for p in range(lane_blocks)], axis=1
                )
            )
        half_out[slot] = jnp.concatenate(bands, axis=0) if len(bands) > 1 else bands[0]
        swap = remote(
            half_out.at[slot], half_in.at[slot],
            pair_send.at[2 + slot], pair_recv.at[2 + slot], sibling,
        )
        swap.start()
        swap.wait()
        lower, upper = half_out[slot], half_in[slot]
        low = jnp.where(core == 0, lower, upper)
        high = jnp.where(core == 0, upper, lower)
        return jnp.concatenate([low, high], axis=0)

    def pack(value):
        return jnp.concatenate([value[: half // 2], value[half // 2 :]], axis=1)

    def gram_sum(value, beside):
        local = mm_nt(value, value)
        gram_out[0] = pack(local[:half])
        gram_out[1] = pack(local[half:])
        swap = remote(
            gram_out.at[1 - core], gram_pair, pair_send.at[4], pair_recv.at[4], sibling
        )
        swap.start()
        swap.wait()
        gram_all[0, chip_me] = gram_out[core] + gram_pair[...]
        mine = gram_all.at[0, chip_me]
        gram_copies = start_chips(0, lambda target: mine, mine, g_send, g_recv)
        beside()
        finish(gram_copies)
        gram_half[...] = chip_sum(gram_all, 0) * inv_total
        swap = remote(gram_half, gram_back, pair_send.at[5], pair_recv.at[5], sibling)
        swap.start()
        swap.wait()
        low = jnp.where(core == 0, gram_half[...], gram_back[...])
        high = jnp.where(core == 0, gram_back[...], gram_half[...])
        return jnp.concatenate([low[:, :cols], low[:, cols:], high[:, :cols], high[:, cols:]], axis=0)

    proj_first = project(0, image_t)
    remainder = image_t - mm_nt(proj_first, basis[...], HIGH)
    proj_second = project(1, remainder)
    second = remainder - mm_nt(proj_second, basis[...], HIGH)
    group = core * n_col + col
    second_copies = []
    pair_copies = []

    def spread():
        second_all[group] = encode(second)
        for j in range(1, n_col):
            mine = second_all.at[group]
            second_copies.append(
                remote(mine, mine, s_send.at[j], s_recv.at[j], col_device(j)[1])
            )
            second_copies[-1].start()
        coef = proj_first + proj_second
        coef_ref[...] = jnp.where(core == 0, coef[:half], coef[half:])

    def share():
        finish(second_copies)
        for c in range(n_col):
            region = second_all.at[core * n_col + c]
            pair_copies.append(remote(region, region, o_send.at[c], o_recv.at[c], sibling))
            pair_copies[-1].start()

    gram = gram_sum(second, spread)
    share()
    upper, inverse = factor(jnp.concatenate([gram, gram], axis=1))
    tri_ref[...] = upper
    own_rows = jnp.where(core == 0, inverse[:half], inverse[half:])
    finish(pair_copies)
    for q in range(pieces):
        new_ref[:, q * piece : (q + 1) * piece] = mm(own_rows, decode(second_all[q]))


def hand_over(new_in, coef_in, tri_in, new_ref, coef_ref, tri_ref):
    new_ref[...] = new_in[...]
    coef_ref[...] = coef_in[...]
    tri_ref[...] = tri_in[...]


def per_device(matrix_panel, start_block, stored_basis):
    n_row = lax.axis_size("row")
    n_col = lax.axis_size("col")
    n_core = lax.axis_size("depth")
    rows_here, cols_here = matrix_panel.shape
    half = start_block.shape[1]
    cols = half * n_core
    k_total = stored_basis.shape[1]
    width = LANES * n_row
    chunks = cols_here // n_core // width
    pieces = n_col * n_core
    piece = rows_here // pieces
    n_chip = n_row * n_col
    piece_lanes = LANES
    piece_rows = half * k_total // (n_chip * piece_lanes)
    dma = pltpu.SemaphoreType.DMA
    bf16 = jnp.bfloat16
    scratch = [
        pltpu.VMEM((chunks, rows_here, width), bf16),
        pltpu.VMEM((n_core, half, rows_here), bf16),
        pltpu.VMEM((n_row, cols, LANES), F32),
        pltpu.VMEM((chunks, cols, LANES), F32),
        pltpu.VMEM((chunks, n_row, cols, LANES), bf16),
        pltpu.VMEM((chunks, n_row, cols, LANES), bf16),
        pltpu.VMEM((chunks, n_row, cols, LANES), bf16),
        pltpu.VMEM((pieces, cols, piece), F32),
        pltpu.VMEM((n_col, cols, piece), F32),
        pltpu.VMEM((n_col, cols, piece), F32),
        pltpu.VMEM((piece, k_total), F32),
        pltpu.VMEM((2, n_core, half, k_total), F32),
        pltpu.VMEM((2, half, k_total), F32),
        pltpu.VMEM((n_chip, piece_rows, piece_lanes), F32),
        pltpu.VMEM((2, n_chip, piece_rows, piece_lanes), F32),
        pltpu.VMEM((2, n_chip, piece_rows, piece_lanes), F32),
        pltpu.VMEM((2, half, k_total), F32),
        pltpu.VMEM((2, half, k_total), F32),
        pltpu.VMEM((n_core, half // 2, 2 * cols), F32),
        pltpu.VMEM((half // 2, 2 * cols), F32),
        pltpu.VMEM((1, n_chip, half // 2, 2 * cols), F32),
        pltpu.VMEM((half // 2, 2 * cols), F32),
        pltpu.VMEM((half // 2, 2 * cols), F32),
        pltpu.VMEM((pieces, cols, piece), bf16),
        dma((chunks,)),
        dma((2,)),
        dma((2,)),
    ]
    scratch += [dma((n_row, chunks))] * 4
    scratch += [dma((n_col,))] * 4
    scratch += [dma((6,))] * 2
    scratch += [dma((2, n_chip))] * 4
    scratch += [dma((1, n_chip))] * 2
    scratch += [dma((n_col,))] * 4
    whole = pl.BlockSpec(memory_space=pltpu.VMEM)
    hbm = pl.BlockSpec(memory_space=pl.ANY)
    shapes = (
        jax.ShapeDtypeStruct((half, rows_here), F32),
        jax.ShapeDtypeStruct((half, k_total), F32),
        jax.ShapeDtypeStruct((cols, cols), F32),
    )
    made = pl.pallas_call(
        functools.partial(krylov_kernel, (n_row, n_col, rows_here * n_row)),
        out_shape=shapes,
        in_specs=[hbm, whole, hbm],
        out_specs=(whole, whole, whole),
        scratch_shapes=scratch,
        compiler_params=pltpu.CompilerParams(
            collective_id=0, has_side_effects=True, vmem_limit_bytes=63 << 20
        ),
    )(matrix_panel, start_block.T, stored_basis)
    new_t, coef_t, triangle = pl.pallas_call(
        hand_over,
        out_shape=shapes,
        in_specs=[whole, whole, whole],
        out_specs=(whole, whole, whole),
    )(*made)
    return (new_t.T, coef_t.T, triangle)


def solution(mesh):
    placed = (P("row", "col"), P("row", "depth"), P("row", None))
    return jax.shard_map(
        per_device,
        mesh=mesh,
        in_specs=placed,
        out_specs=(P("row", "depth"), P(None, "depth"), P()),
        check_vma=False,
    )
```

```python
import functools

import jax
import jax.numpy as jnp
from jax import lax
from jax.experimental import pallas as pl
from jax.experimental.pallas import tpu as pltpu
from jax.sharding import PartitionSpec as P

HIGHEST = lax.Precision.HIGHEST
HIGH = lax.Precision.HIGH
MESH = pl.DeviceIdType.MESH
F32 = jnp.float32
LANES = 128
LAG_SUM = 5
LAG_USE = 12
LATE = 4


def mm(a, b, precision=HIGHEST):
    return lax.dot_general(
        a, b, (((1,), (0,)), ((), ())), precision=precision, preferred_element_type=F32
    )


def mm_nt(a, b, precision=HIGHEST):
    return lax.dot_general(
        a, b, (((1,), (1,)), ((), ())), precision=precision, preferred_element_type=F32
    )


def factor(gram_twice):
    size = gram_twice.shape[0]
    rows = lax.broadcasted_iota(jnp.int32, (size, 2 * size), 0)
    lanes = lax.broadcasted_iota(jnp.int32, (size, 2 * size), 1)
    work = jnp.where(lanes < size, gram_twice, jnp.where(lanes - size == rows, 1.0, 0.0))

    def all_sum(mask, value):
        part_sum = jnp.sum(jnp.where(mask, value, 0.0), axis=0, keepdims=True)
        return jnp.sum(part_sum, axis=1, keepdims=True)

    def step(i, carry):
        work, pivots = carry
        k = 2 * i
        n = k + 1
        lane_k, lane_n = lanes == k, lanes == n
        row_is_k, row_is_n = rows == k, rows == n
        column_k = jnp.sum(jnp.where(lane_k, work, 0.0), axis=1, keepdims=True)
        column_n = jnp.sum(jnp.where(lane_n, work, 0.0), axis=1, keepdims=True)
        row_k = jnp.sum(jnp.where(row_is_k, work, 0.0), axis=0, keepdims=True)
        row_n = jnp.sum(jnp.where(row_is_n, work, 0.0), axis=0, keepdims=True)
        pivot_k = all_sum(row_is_k & lane_k, work)
        upper = all_sum(row_is_k & lane_n, work)
        lower = all_sum(row_is_n & lane_k, work)
        corner = all_sum(row_is_n & lane_n, work)
        ratio = lower / pivot_k
        pivot_n = corner - ratio * upper
        row_n = row_n - ratio * row_k
        scale_k = column_k / pivot_k
        scale_n = (column_n - scale_k * upper) / pivot_n
        work = work - jnp.where(rows > k, scale_k * row_k, 0.0)
        work = work - jnp.where(rows > n, scale_n * row_n, 0.0)
        pivots = jnp.where(row_is_k, pivot_k, jnp.where(row_is_n, pivot_n, pivots))
        return (work, pivots)

    work, pivots = lax.fori_loop(0, size // 2, step, (work, jnp.ones_like(work)))
    work = work / jnp.sqrt(pivots)
    upper = jnp.where(rows <= lanes, work, 0.0)[:, :size]
    return (upper, work[:, size:])


def encode(value):
    return (value * jnp.abs(value)).astype(jnp.bfloat16)


def decode(code):
    code = code.astype(F32)
    return code * lax.rsqrt(jnp.maximum(jnp.abs(code), 1e-37))


def krylov_kernel(
    dims,
    panel_ref,
    start_ref,
    basis_ref,
    new_ref,
    coef_ref,
    tri_ref,
    held,
    start_all,
    fresh,
    own,
    part,
    landed,
    gathered,
    image,
    sib_buf,
    col_buf,
    basis,
    pair_out,
    pair_in,
    proj_part,
    proj_in,
    proj_all,
    half_out,
    half_in,
    gram_out,
    gram_pair,
    gram_all,
    gram_half,
    gram_back,
    second_all,
    panel_sem,
    misc_sem,
    sib_sem,
    r_send,
    r_recv,
    b_send,
    b_recv,
    half_send,
    half_recv,
    col_send,
    col_recv,
    pair_send,
    pair_recv,
    p_send,
    p_recv,
    a_send,
    a_recv,
    g_send,
    g_recv,
    o_send,
    o_recv,
    s_send,
    s_recv,
):
    n_row, n_col, total_rows = dims
    chunks, rows_here, width = held.shape
    cols = start_all.shape[0] * start_all.shape[1]
    half = cols // 2
    pieces = image.shape[0]
    piece = image.shape[2]
    n_chip = n_row * n_col
    row = lax.axis_index("row")
    col = lax.axis_index("col")
    core = lax.axis_index("depth")
    inv_total = 1.0 / total_rows
    chip_me = row * n_col + col
    sibling = {"depth": 1 - core}

    def chip_device(j):
        target = (chip_me + j) % n_chip
        return target, {"row": target // n_col, "col": target % n_col}

    def col_device(j):
        target = (col + j) % n_col
        return target, {"col": target}

    def row_device(j):
        target = (row + j) % n_row
        return target, {"row": target}

    def panel_copy(t):
        first = pl.multiple_of((core * chunks + t) * width, width)
        return pltpu.make_async_copy(
            panel_ref.at[:, pl.ds(first, width)], held.at[t], panel_sem.at[t]
        )

    own_start = pltpu.make_async_copy(start_ref, start_all.at[core], misc_sem.at[1])
    own_start.start()
    for t in range(chunks):
        panel_copy(t).start()
    basis_first = pl.multiple_of((core * n_col + col) * piece, 8)
    basis_copy = pltpu.make_async_copy(
        basis_ref.at[pl.ds(basis_first, piece), :], basis, misc_sem.at[0]
    )
    basis_copy.start()

    barrier = pltpu.get_barrier_semaphore()
    greeted = [row_device(j)[1] for j in range(1, n_row)]
    greeted += [col_device(j)[1] for j in range(1, n_col)] + [sibling]
    for device in greeted:
        pl.semaphore_signal(barrier, inc=1, device_id=device, device_id_type=MESH)
    pl.semaphore_wait(barrier, len(greeted))

    def remote(src, dst, send_sem, recv_sem, device):
        return pltpu.make_async_remote_copy(
            src_ref=src,
            dst_ref=dst,
            send_sem=send_sem,
            recv_sem=recv_sem,
            device_id=device,
            device_id_type=MESH,
        )

    start_copy = remote(start_ref, start_all.at[core], sib_sem.at[0], sib_sem.at[1], sibling)
    start_copy.start()
    image[...] = jnp.zeros_like(image)
    own_start.wait()
    start_copy.wait()

    def reduce_copy(j, t):
        target, device = row_device(j)
        return remote(
            part.at[t, target], landed.at[t, row], r_send.at[j, t], r_recv.at[j, t], device
        )

    def gather_copy(j, t):
        region = gathered.at[t, row]
        return remote(region, region, b_send.at[j, t], b_recv.at[j, t], row_device(j)[1])

    def multiply(i):
        panel_copy(i).wait()
        mixed = mm(start_all[...].reshape(cols, rows_here), held[i], None)
        for p in range(n_row):
            lanes = mixed[:, p * LANES : (p + 1) * LANES]
            fresh[p] = lanes
            part[i, p] = encode(lanes)
        for j in range(1, n_row):
            reduce_copy(j, i).start()
        own[i] = fresh[row]

    def combine(t):
        for j in range(1, n_row):
            reduce_copy(j, t).wait_recv()
        summed = own[t]
        for j in range(1, n_row):
            summed = summed + decode(landed[t, (row + j) % n_row])
        gathered[t, row] = summed.astype(jnp.bfloat16)
        for j in range(1, n_row):
            gather_copy(j, t).start()

    block = rows_here // 4
    per_block = block // piece

    def mixed_of(t):
        for j in range(1, n_row):
            gather_copy(j, t).wait_recv()
        return jnp.concatenate([gathered[t, p] for p in range(n_row)], axis=1)

    def apply(t):
        lhs = mixed_of(t)
        for h in range(4):
            got = mm_nt(lhs, held[t, h * block : (h + 1) * block, :], None)
            for q in range(per_block):
                image[h * per_block + q] += got[:, q * piece : (q + 1) * piece]

    early = max(chunks - LATE, 0)
    cuts = sorted({0, LAG_SUM, LAG_USE, chunks, chunks + LAG_SUM, early + LAG_USE})
    for first, last in zip(cuts[:-1], cuts[1:]):

        def body(i, carry, first=first):
            if LAG_SUM <= first < chunks + LAG_SUM:
                combine(i - LAG_SUM)
            if first < chunks:
                multiply(i)
            if LAG_USE <= first:
                apply(i - LAG_USE)
            return carry

        lax.fori_loop(first, last, body, 0)

    def half_copy(c):
        return remote(
            image.at[(1 - core) * n_col + c], sib_buf.at[c], half_send.at[c], half_recv.at[c], sibling
        )

    late = [(t, mixed_of(t)) for t in range(early, chunks)]

    def finish_piece(index):
        first = pl.multiple_of(index * piece, 16)
        got = image[index]
        for t, lhs in late:
            got = got + mm_nt(lhs, held[t, pl.ds(first, piece), :], None)
        image[index] = got

    def pass_on(j):
        target = (col + j) % n_col
        finish_piece((1 - core) * n_col + target)
        half_copy(target).start()

    pass_on(1)
    copies = []
    for j in range(1, n_col):
        target, device = col_device(j)
        pass_on(j + 1)
        finish_piece(core * n_col + target)
        half_copy(target).wait_recv()
        sib_buf[target] = sib_buf[target] + image[core * n_col + target]
        copies.append(
            remote(sib_buf.at[target], col_buf.at[col], col_send.at[j], col_recv.at[j], device)
        )
        copies[-1].start()
    finish_piece(core * n_col + col)
    half_copy(col).wait_recv()
    col_buf[col] = sib_buf[col] + image[core * n_col + col]

    def drain(t, carry):
        for j in range(1, n_row):
            reduce_copy(j, t).wait_send()
            gather_copy(j, t).wait_send()
        return carry

    lax.fori_loop(0, chunks, drain, 0)
    for c in range(n_col):
        half_copy(c).wait_send()
    basis_copy.wait()
    for copy in copies:
        copy.wait()

    image_t = col_buf[0]
    for c in range(1, n_col):
        image_t = image_t + col_buf[c]

    piece_rows, piece_lanes = proj_part.shape[1:]
    lane_blocks = basis.shape[1] // piece_lanes

    def finish(made):
        for copy in made:
            copy.wait()

    def start_chips(slot, src_of, dst, send, recv):
        made = []
        for j in range(1, n_chip):
            target, device = chip_device(j)
            made.append(remote(src_of(target), dst, send.at[slot, j], recv.at[slot, j], device))
            made[-1].start()
        return made

    def chip_sum(ref, slot):
        total = ref[slot, 0]
        for c in range(1, n_chip):
            total = total + ref[slot, c]
        return total

    def project(slot, value):
        partial = mm(value, basis[...], HIGH)
        pair_out[slot, 0] = partial[:half]
        pair_out[slot, 1] = partial[half:]
        swap = remote(
            pair_out.at[slot, 1 - core], pair_in.at[slot],
            pair_send.at[slot], pair_recv.at[slot], sibling,
        )
        swap.start()
        swap.wait()
        both = pair_out[slot, core] + pair_in[slot]
        for p in range(n_chip):
            lane = (p % lane_blocks) * piece_lanes
            top = (p // lane_blocks) * piece_rows
            proj_part[p] = both[top : top + piece_rows, lane : lane + piece_lanes]
        copies = start_chips(
            slot, lambda target: proj_part.at[target], proj_in.at[slot, chip_me], p_send, p_recv
        )
        proj_in[slot, chip_me] = proj_part[chip_me]
        finish(copies)
        proj_all[slot, chip_me] = chip_sum(proj_in, slot) * inv_total
        mine = proj_all.at[slot, chip_me]
        finish(start_chips(slot, lambda target: mine, mine, a_send, a_recv))
        bands = []
        for top in range(n_chip // lane_blocks):
            bands.append(
                jnp.concatenate(
                    [proj_all[slot, top * lane_blocks + p] for p in range(lane_blocks)], axis=1
                )
            )
        half_out[slot] = jnp.concatenate(bands, axis=0) if len(bands) > 1 else bands[0]
        swap = remote(
            half_out.at[slot], half_in.at[slot],
            pair_send.at[2 + slot], pair_recv.at[2 + slot], sibling,
        )
        swap.start()
        swap.wait()
        lower, upper = half_out[slot], half_in[slot]
        low = jnp.where(core == 0, lower, upper)
        high = jnp.where(core == 0, upper, lower)
        return jnp.concatenate([low, high], axis=0)

    def pack(value):
        return jnp.concatenate([value[: half // 2], value[half // 2 :]], axis=1)

    def gram_sum(value, beside):
        local = mm_nt(value, value)
        gram_out[0] = pack(local[:half])
        gram_out[1] = pack(local[half:])
        swap = remote(
            gram_out.at[1 - core], gram_pair, pair_send.at[4], pair_recv.at[4], sibling
        )
        swap.start()
        swap.wait()
        gram_all[0, chip_me] = gram_out[core] + gram_pair[...]
        mine = gram_all.at[0, chip_me]
        gram_copies = start_chips(0, lambda target: mine, mine, g_send, g_recv)
        beside()
        finish(gram_copies)
        gram_half[...] = chip_sum(gram_all, 0) * inv_total
        swap = remote(gram_half, gram_back, pair_send.at[5], pair_recv.at[5], sibling)
        swap.start()
        swap.wait()
        low = jnp.where(core == 0, gram_half[...], gram_back[...])
        high = jnp.where(core == 0, gram_back[...], gram_half[...])
        return jnp.concatenate([low[:, :cols], low[:, cols:], high[:, :cols], high[:, cols:]], axis=0)

    proj_first = project(0, image_t)
    remainder = image_t - mm_nt(proj_first, basis[...], HIGH)
    proj_second = project(1, remainder)
    second = remainder - mm_nt(proj_second, basis[...], HIGH)
    group = core * n_col + col
    second_copies = []
    pair_copies = []

    def spread():
        second_all[group] = encode(second)
        for j in range(1, n_col):
            mine = second_all.at[group]
            second_copies.append(
                remote(mine, mine, s_send.at[j], s_recv.at[j], col_device(j)[1])
            )
            second_copies[-1].start()
        coef = proj_first + proj_second
        coef_ref[...] = jnp.where(core == 0, coef[:half], coef[half:])

    def share():
        finish(second_copies)
        for c in range(n_col):
            region = second_all.at[core * n_col + c]
            pair_copies.append(remote(region, region, o_send.at[c], o_recv.at[c], sibling))
            pair_copies[-1].start()

    gram = gram_sum(second, spread)
    share()
    upper, inverse = factor(jnp.concatenate([gram, gram], axis=1))
    tri_ref[...] = upper
    own_rows = jnp.where(core == 0, inverse[:half], inverse[half:])
    finish(pair_copies)
    for q in range(pieces):
        new_ref[:, q * piece : (q + 1) * piece] = mm(own_rows, decode(second_all[q]))


def hand_over(new_in, coef_in, tri_in, new_ref, coef_ref, tri_ref):
    new_ref[...] = new_in[...]
    coef_ref[...] = coef_in[...]
    tri_ref[...] = tri_in[...]


def per_device(matrix_panel, start_block, stored_basis):
    n_row = lax.axis_size("row")
    n_col = lax.axis_size("col")
    n_core = lax.axis_size("depth")
    rows_here, cols_here = matrix_panel.shape
    half = start_block.shape[1]
    cols = half * n_core
    k_total = stored_basis.shape[1]
    width = LANES * n_row
    chunks = cols_here // n_core // width
    pieces = n_col * n_core
    piece = rows_here // pieces
    n_chip = n_row * n_col
    piece_lanes = LANES
    piece_rows = half * k_total // (n_chip * piece_lanes)
    dma = pltpu.SemaphoreType.DMA
    bf16 = jnp.bfloat16
    scratch = [
        pltpu.VMEM((chunks, rows_here, width), bf16),
        pltpu.VMEM((n_core, half, rows_here), bf16),
        pltpu.VMEM((n_row, cols, LANES), F32),
        pltpu.VMEM((chunks, cols, LANES), F32),
        pltpu.VMEM((chunks, n_row, cols, LANES), bf16),
        pltpu.VMEM((chunks, n_row, cols, LANES), bf16),
        pltpu.VMEM((chunks, n_row, cols, LANES), bf16),
        pltpu.VMEM((pieces, cols, piece), F32),
        pltpu.VMEM((n_col, cols, piece), F32),
        pltpu.VMEM((n_col, cols, piece), F32),
        pltpu.VMEM((piece, k_total), F32),
        pltpu.VMEM((2, n_core, half, k_total), F32),
        pltpu.VMEM((2, half, k_total), F32),
        pltpu.VMEM((n_chip, piece_rows, piece_lanes), F32),
        pltpu.VMEM((2, n_chip, piece_rows, piece_lanes), F32),
        pltpu.VMEM((2, n_chip, piece_rows, piece_lanes), F32),
        pltpu.VMEM((2, half, k_total), F32),
        pltpu.VMEM((2, half, k_total), F32),
        pltpu.VMEM((n_core, half // 2, 2 * cols), F32),
        pltpu.VMEM((half // 2, 2 * cols), F32),
        pltpu.VMEM((1, n_chip, half // 2, 2 * cols), F32),
        pltpu.VMEM((half // 2, 2 * cols), F32),
        pltpu.VMEM((half // 2, 2 * cols), F32),
        pltpu.VMEM((pieces, cols, piece), bf16),
        dma((chunks,)),
        dma((2,)),
        dma((2,)),
    ]
    scratch += [dma((n_row, chunks))] * 4
    scratch += [dma((n_col,))] * 4
    scratch += [dma((6,))] * 2
    scratch += [dma((2, n_chip))] * 4
    scratch += [dma((1, n_chip))] * 2
    scratch += [dma((n_col,))] * 4
    whole = pl.BlockSpec(memory_space=pltpu.VMEM)
    hbm = pl.BlockSpec(memory_space=pl.ANY)
    shapes = (
        jax.ShapeDtypeStruct((half, rows_here), F32),
        jax.ShapeDtypeStruct((half, k_total), F32),
        jax.ShapeDtypeStruct((cols, cols), F32),
    )
    made = pl.pallas_call(
        functools.partial(krylov_kernel, (n_row, n_col, rows_here * n_row)),
        out_shape=shapes,
        in_specs=[hbm, whole, hbm],
        out_specs=(whole, whole, whole),
        scratch_shapes=scratch,
        compiler_params=pltpu.CompilerParams(
            collective_id=0, has_side_effects=True, vmem_limit_bytes=63 << 20
        ),
    )(matrix_panel, start_block.T, stored_basis)
    new_t, coef_t, triangle = pl.pallas_call(
        hand_over,
        out_shape=shapes,
        in_specs=[whole, whole, whole],
        out_specs=(whole, whole, whole),
    )(*made)
    return (new_t.T, coef_t.T, triangle)


def solution(mesh):
    placed = (P("row", "col"), P("row", "depth"), P("row", None))
    return jax.shard_map(
        per_device,
        mesh=mesh,
        in_specs=placed,
        out_specs=(P("row", "depth"), P(None, "depth"), P()),
        check_vma=False,
    )
```
